512 devices in a mesh: layer: 32 (over z, core), dp: 16 (over x, y).
Axes of the slice: x: 4, y: 4, z: 16, core: 2. Of those that a mesh axis runs over, the one named last changes fastest.
Arguments:
- states: bfloat16 [32, 2048, 512], P('layer', 'dp'), may hold values from -6 to 6
- w_in: bfloat16 [64, 512, 1024], P('layer'), may hold values from -0.25 to 0.25
- w_out: bfloat16 [64, 1024, 512], P('layer'), may hold values from -0.1875 to 0.1875
Outputs:
- c_states: bfloat16 [32, 2048, 512], P('layer', 'dp')
- f_states: bfloat16 [32, 2048, 512], P('layer', 'dp')
The draws below stay inside these ranges and needn't reach their ends.
All inputs are finite; a program needn't handle non-finite values.
Results may differ from the reference program's by a relative error of at most 0.018.
Values may be sent and summed in bfloat16 or wider, within the bound.
A program may use at most 128 MiB of HBM per device.

```python
import jax
import jax.numpy as jnp
from jax import lax

D = 512
H = 1024
COARSE = 32
LAYERS = 64
TOKENS = 2048


def steps_of(key, shape, shards, smallest, high):
    def one(axis_at, parts):
        heights = jax.random.uniform(jax.random.fold_in(jax.random.fold_in(key, 6), axis_at), (parts,), jnp.float32, smallest / len(shards), high / len(shards))
        return jnp.repeat(jnp.exp(heights), shape[axis_at] // parts).reshape((-1,) + (1,) * (len(shape) - axis_at - 1))

    factor_of = one(*shards[0])
    for cut in shards[1:]:
        factor_of = factor_of * one(*cut)
    return factor_of


def gaussian(stream_key, dims, scale, most, cuts=(), kind=jnp.bfloat16):
    values = jax.random.normal(stream_key, dims, jnp.float32) * scale
    if len(cuts) > 0:
        values = steps_of(stream_key, dims, cuts, -0.22, 0.18) * values
    return jnp.clip(values, min=-most, max=most).astype(kind)


def setup_inputs(seed: int = 0) -> dict:
    key_list = jax.random.split(jax.random.key(seed), 4)
    states = gaussian(key_list[0], (COARSE, TOKENS, D), 1.0, 6.0, ((0, 32), (1, 16)))
    w_in = gaussian(key_list[1], (LAYERS, D, H), D ** -0.5, 0.25, ((0, 32),))
    w_out = gaussian(key_list[2], (LAYERS, H, D), H ** -0.5, 0.1875, ((0, 32),))
    return {"states": states, "w_in": w_in, "w_out": w_out}


def advance(state, w_first, w_second):
    inner = jnp.dot(state, w_first, preferred_element_type=jnp.float32)
    gated = jax.nn.gelu(inner, approximate=False).astype(jnp.bfloat16)
    branch = jnp.dot(gated, w_second, preferred_element_type=jnp.float32)
    return (state.astype(jnp.float32) + 0.25 * branch).astype(jnp.bfloat16)


def apply_all(stack, w_first, w_second):
    return lax.map(lambda item: advance(item[0], item[1], item[2]), (stack, w_first, w_second))


def reference(states, w_in, w_out):
    even_in, even_out = w_in[0::2], w_out[0::2]
    odd_in, odd_out = w_in[1::2], w_out[1::2]
    relaxed_f = apply_all(states, even_in, even_out)
    pushed = apply_all(relaxed_f, odd_in, odd_out)
    following = jnp.concatenate([states[1:].astype(jnp.float32), jnp.zeros((1, TOKENS, D), jnp.float32)], axis=0)
    defect = pushed.astype(jnp.float32) - following
    identity = jnp.eye(D, dtype=jnp.float32)

    def make_map(item):
        return identity + 0.25 * jnp.dot(item[0], item[1], preferred_element_type=jnp.float32)

    coarse_map = lax.map(make_map, (even_in, even_out))

    def step_fn(carry, item):
        nxt = jnp.dot(carry, item[0], precision=lax.Precision.HIGHEST, preferred_element_type=jnp.float32) + item[1]
        return nxt, carry

    start = jnp.zeros((TOKENS, D), jnp.float32)
    _, correction = lax.scan(step_fn, start, (coarse_map, defect))
    c_states = (states.astype(jnp.float32) + correction).astype(jnp.bfloat16)
    f_states = apply_all(c_states, even_in, even_out)
    return c_states, f_states
```

```python
import functools

import jax
import jax.numpy as jnp
from jax import lax
from jax.experimental import pallas as pl
from jax.experimental.pallas import tpu as pltpu
from jax.sharding import PartitionSpec as P

F32, BF16 = jnp.float32, jnp.bfloat16
ROOT_HALF = 0.7071067811865476
CHUNKS = 2


def dot(left, right):
    return jnp.dot(left, right, preferred_element_type=F32)


def gelu(x):
    return 0.5 * x * (1.0 + lax.erf(x * ROOT_HALF))


def advance(state, w_first, w_second):
    gated = gelu(dot(state, w_first)).astype(BF16)
    return (state.astype(F32) + 0.25 * dot(gated, w_second)).astype(BF16)


def kernel(
    layers, states_ref, win_hbm, wout_hbm, c_ref, f_ref,
    win, wout, follow, maps, pair, defect, half_out, half_in, d_all, b_half, carried, leaving,
    load_sem, follow_sems, map_sems, half_sems, chain_send, chain_recv, share_send, share_recv,
):
    me = lax.axis_index("layer")
    core = lax.rem(me, 2)
    partner = me + 1 - 2 * core
    first, last = me < 2, me >= layers - 2
    rows = states_ref.shape[0]
    half = rows // 2
    step = half // CHUNKS
    mine = core * half

    loads = []
    for at in range(2):
        for source, target, slot in ((win_hbm, win, 2 * at), (wout_hbm, wout, 2 * at + 1)):
            load = pltpu.make_async_copy(source.at[at], target.at[at], load_sem.at[slot])
            load.start()
            loads.append(load)

    barrier = pltpu.get_barrier_semaphore()

    def greet(device):
        pl.semaphore_signal(barrier, inc=1, device_id={"layer": device})

    greet(partner)
    beside = me - 1 + 2 * core
    has_beside = jnp.logical_and(beside >= 0, beside < layers)

    @pl.when(has_beside)
    def _():
        greet(beside)

    @pl.when(jnp.logical_not(first))
    def _():
        greet(me - 2)

    @pl.when(jnp.logical_not(last))
    def _():
        greet(me + 2)

    expected = 1 + has_beside.astype(jnp.int32) + (me >= 2).astype(jnp.int32) + (me < layers - 2).astype(jnp.int32)
    pl.semaphore_wait(barrier, expected)

    def remote(source, target, send, recv, device):
        return pltpu.make_async_remote_copy(
            src_ref=source, dst_ref=target, send_sem=send, recv_sem=recv, device_id={"layer": device}
        )

    to_before = remote(states_ref, follow, follow_sems.at[0], follow_sems.at[1], me - 1)

    @pl.when(me > 0)
    def _():
        to_before.start()

    loads[0].wait()
    loads[1].wait()
    width = win.shape[1]
    own_map = maps.at[core]
    own_map[...] = (0.25 * dot(win[0], wout[0])).astype(BF16)
    share_map = remote(own_map, own_map, map_sems.at[0], map_sems.at[1], partner)
    share_map.start()

    state = states_ref[...]
    relaxed = advance(state, win[0], wout[0])
    loads[2].wait()
    loads[3].wait()
    pushed = advance(relaxed, win[1], wout[1])

    @pl.when(me < layers - 1)
    def _():
        to_before.wait_recv()

    @pl.when(me == layers - 1)
    def _():
        follow[...] = jnp.zeros_like(follow)

    defect[...] = pushed.astype(F32) - follow[...].astype(F32)
    half_out[...] = defect[...].astype(BF16)
    share_half = remote(half_out, half_in, half_sems.at[0], half_sems.at[1], partner)
    share_half.start()

    share_map.wait_recv()
    even_map, odd_map = maps[0], maps[1]
    pair[...] = (even_map.astype(F32) + odd_map.astype(F32) + dot(even_map, odd_map)).astype(BF16)
    share_half.wait_recv()

    own_rows = pl.ds(pl.multiple_of(mine, half), half)

    @pl.when(core == 0)
    def _():
        d_all[...] = defect[...]
        b_half[...] = half_in[own_rows, :].astype(F32)

    @pl.when(core == 1)
    def _():
        d_all[...] = half_in[...].astype(F32)
        b_half[...] = defect[own_rows, :]

    even_half = d_all[own_rows, :]
    b_half[...] += even_half + dot(even_half.astype(BF16), maps[1])

    @pl.when(first)
    def _():
        carried[...] = jnp.zeros_like(carried)

    def chunk(at):
        return pl.ds(pl.multiple_of(mine + at * step, step), step)

    hops, shares = [], []
    for at in range(CHUNKS):
        piece = leaving.at[pl.ds(at * step, step), :]
        hops.append(remote(piece, carried.at[chunk(at), :], chain_send.at[at], chain_recv.at[at], me + 2))
        block = carried.at[chunk(at), :]
        shares.append(remote(block, block, share_send.at[at], share_recv.at[at], partner))

    for at in range(CHUNKS):
        @pl.when(jnp.logical_not(first))
        def _(at=at):
            hops[at].wait_recv()
            shares[at].start()

        @pl.when(jnp.logical_not(last))
        def _(at=at):
            here = carried[chunk(at), :]
            ahead = here.astype(F32) + dot(here, pair[...]) + b_half[pl.ds(at * step, step), :]
            leaving[pl.ds(at * step, step), :] = ahead.astype(BF16)
            hops[at].start()

    @pl.when(jnp.logical_not(first))
    def _():
        for share in shares:
            share.wait_recv()

    @pl.when(core == 0)
    def _():
        c_ref[...] = (states_ref[...].astype(F32) + carried[...].astype(F32)).astype(BF16)

    @pl.when(core == 1)
    def _():
        here = carried[...]
        correction = here.astype(F32) + dot(here, maps[0]) + d_all[...]
        c_ref[...] = (states_ref[...].astype(F32) + correction).astype(BF16)

    f_ref[...] = advance(c_ref[...], win[0], wout[0])

    @pl.when(me > 0)
    def _():
        to_before.wait_send()

    share_map.wait_send()
    share_half.wait_send()

    @pl.when(jnp.logical_not(first))
    def _():
        for share in shares:
            share.wait_send()

    @pl.when(jnp.logical_not(last))
    def _():
        for hop in hops:
            hop.wait_send()


def shards(layers, states, w_in, w_out):
    rows, width = states.shape[1:]
    hidden = w_in.shape[2]
    half = rows // 2
    block = jax.ShapeDtypeStruct((rows, width), BF16)
    vmem = pl.BlockSpec(memory_space=pltpu.VMEM)
    hbm = pl.BlockSpec(memory_space=pl.ANY)
    dma = pltpu.SemaphoreType.DMA
    corrected, fine = pl.pallas_call(
        functools.partial(kernel, layers),
        out_shape=(block, block),
        in_specs=[vmem, hbm, hbm],
        out_specs=(vmem, vmem),
        scratch_shapes=[
            pltpu.VMEM((2, width, hidden), BF16),
            pltpu.VMEM((2, hidden, width), BF16),
            pltpu.VMEM((rows, width), BF16),
            pltpu.VMEM((2, width, width), BF16),
            pltpu.VMEM((width, width), BF16),
            pltpu.VMEM((rows, width), F32),
            pltpu.VMEM((rows, width), BF16),
            pltpu.VMEM((rows, width), BF16),
            pltpu.VMEM((rows, width), F32),
            pltpu.VMEM((half, width), F32),
            pltpu.VMEM((rows, width), BF16),
            pltpu.VMEM((half, width), BF16),
            dma((4,)),
            dma((2,)),
            dma((2,)),
            dma((2,)),
            dma((CHUNKS,)),
            dma((CHUNKS,)),
            dma((CHUNKS,)),
            dma((CHUNKS,)),
        ],
        compiler_params=pltpu.CompilerParams(
            collective_id=0, has_side_effects=True, vmem_limit_bytes=48 * 1024 * 1024
        ),
    )(states[0], w_in, w_out)
    return (corrected[None], fine[None])


def solution(mesh):
    return jax.shard_map(
        functools.partial(shards, mesh.shape["layer"]),
        mesh=mesh,
        in_specs=(P("layer", "dp", None), P("layer", None, None), P("layer", None, None)),
        out_specs=(P("layer", "dp", None), P("layer", "dp", None)),
        check_vma=False,
    )
```

```python
import functools

import jax
import jax.numpy as jnp
from jax import lax
from jax.experimental import pallas as pl
from jax.experimental.pallas import tpu as pltpu
from jax.sharding import PartitionSpec as P

F32, BF16 = jnp.float32, jnp.bfloat16
ROOT_HALF = 0.7071067811865476
CHUNKS = 2


def groups_of(chips):
    if chips == 16:
        return (4, 4, 5, 3)
    return tuple([max(1, chips // 3)] * 2 + [chips - 2 * max(1, chips // 3)])


def dot(left, right):
    return jnp.dot(left, right, preferred_element_type=F32)


def gelu(x):
    return 0.5 * x * (1.0 + lax.erf(x * ROOT_HALF))


def advance(state, w_first, w_second):
    gated = gelu(dot(state, w_first)).astype(BF16)
    return (state.astype(F32) + 0.25 * dot(gated, w_second)).astype(BF16)


def kernel(
    layers, columns, states_ref, win_hbm, wout_hbm, c_ref, f_ref,
    win, wout, follow, maps, pair, defect, half_out, half_in, d_all, b_half, carried,
    local_in, local_out, x_in, x_out, prefix, e_in, e_out, c_half,
    load_sem, follow_sems, map_sems, half_sems, x_sems, gather_send, gather_recv, swap_sems,
    local_send, local_recv, e_send, e_recv, share_send, share_recv,
):
    me, column = lax.axis_index("layer"), lax.axis_index("dp")
    core, chip = lax.rem(me, 2), me // 2
    partner = me + 1 - 2 * core
    rows, width = states_ref.shape
    half, half_width = rows // 2, width // 2
    step = half // CHUNKS
    part = half_width // columns
    mine = core * half

    sizes = groups_of(layers // 2)
    widest = max(sizes[1:])
    start, size, following_size, at = 0, sizes[0], sizes[1], 0
    for k in range(1, len(sizes)):
        at += sizes[k - 1]
        reached = (chip >= at).astype(jnp.int32)
        ahead = sizes[k + 1] if k + 1 < len(sizes) else 0
        start = start + reached * sizes[k - 1]
        size = size + reached * (sizes[k] - sizes[k - 1])
        following_size = following_size + reached * (ahead - sizes[k])
    number = lambda flag: flag.astype(jnp.int32)
    opens = chip == start
    closes = chip == start + size - 1
    later = chip >= sizes[0]
    recv_local, send_local = jnp.logical_not(opens), jnp.logical_not(closes)
    recv_x, send_x = jnp.logical_and(recv_local, later), jnp.logical_and(send_local, later)
    send_e = jnp.logical_and(closes, following_size > 0)

    loads = []
    for at in range(2):
        for source, target, slot in ((win_hbm, win, 2 * at), (wout_hbm, wout, 2 * at + 1)):
            load = pltpu.make_async_copy(source.at[at], target.at[at], load_sem.at[slot])
            load.start()
            loads.append(load)

    barrier = pltpu.get_barrier_semaphore()
    send_back = jnp.logical_and(core == 0, me > 0)
    recv_back = jnp.logical_and(core == 1, me < layers - 1)

    def greet(**device):
        pl.semaphore_signal(barrier, inc=1, device_id=device)

    greet(layer=partner)

    @pl.when(recv_back)
    def _():
        greet(layer=me + 1)

    @pl.when(recv_local)
    def _():
        greet(layer=me - 2)

    @pl.when(later)
    def _():
        greet(layer=2 * (start - 1) + core)

    peers = [lax.rem(column + turn, columns) for turn in range(1, columns)]

    @pl.when(recv_x)
    def _():
        for peer in peers:
            greet(dp=peer)

    def remote(source, target, send, recv, **device):
        return pltpu.make_async_remote_copy(
            src_ref=source, dst_ref=target, send_sem=send, recv_sem=recv, device_id=device
        )

    loads[0].wait()
    loads[1].wait()
    own_map = maps.at[core]
    own_map[...] = (0.25 * dot(win[0], wout[0])).astype(BF16)

    pl.semaphore_wait(
        barrier,
        1 + number(send_back) + number(send_local) + number(send_e) * following_size
        + number(recv_x) * (columns - 1),
    )
    share_map = remote(own_map, own_map, map_sems.at[0], map_sems.at[1], layer=partner)
    share_map.start()
    to_before = remote(states_ref, follow, follow_sems.at[0], follow_sems.at[1], layer=me - 1)

    @pl.when(me > 0)
    def _():
        to_before.start()

    state = states_ref[...]
    relaxed = advance(state, win[0], wout[0])

    share_map.wait_recv()
    even_map, odd_map = maps[0], maps[1]
    pair[...] = (even_map.astype(F32) + odd_map.astype(F32) + dot(even_map, odd_map)).astype(BF16)

    own_part = pl.ds(pl.multiple_of(core * half_width + column * part, part), part)
    x_hop = remote(x_out, x_in, x_sems.at[0], x_sems.at[1], layer=me + 2)
    gathers = [
        remote(x_in, prefix.at[own_part, :], gather_send.at[turn], gather_recv, dp=peer)
        for turn, peer in enumerate(peers)
    ]
    half_prefix = prefix.at[pl.ds(pl.multiple_of(core * half_width, half_width), half_width), :]
    swap = remote(half_prefix, half_prefix, swap_sems.at[0], swap_sems.at[1], layer=partner)

    def x_step(received):
        ahead = pair[own_part, :].astype(F32)
        if received:
            x = x_in[...]
            ahead = ahead + x.astype(F32) + dot(x, pair[...])
        x_out[...] = ahead.astype(BF16)
        x_hop.start()

    @pl.when(jnp.logical_and(send_x, opens))
    def _():
        x_step(False)

    loads[2].wait()
    loads[3].wait()
    pushed = advance(relaxed, win[1], wout[1])

    @pl.when(me < layers - 1)
    def _():
        to_before.wait_recv()

    @pl.when(me == layers - 1)
    def _():
        follow[...] = jnp.zeros_like(follow)

    defect[...] = pushed.astype(F32) - follow[...].astype(F32)
    half_out[...] = defect[...].astype(BF16)
    share_half = remote(half_out, half_in, half_sems.at[0], half_sems.at[1], layer=partner)
    share_half.start()
    share_half.wait_recv()

    own_rows = pl.ds(pl.multiple_of(mine, half), half)

    @pl.when(core == 0)
    def _():
        d_all[...] = defect[...]
        b_half[...] = half_in[own_rows, :].astype(F32)

    @pl.when(core == 1)
    def _():
        d_all[...] = half_in[...].astype(F32)
        b_half[...] = defect[own_rows, :]

    even_half = d_all[own_rows, :]
    b_half[...] += even_half + dot(even_half.astype(BF16), maps[1])

    spans = [pl.ds(at * step, step) for at in range(CHUNKS)]
    local_hops = [
        remote(local_out.at[span, :], local_in.at[span, :], local_send.at[at], local_recv.at[at], layer=me + 2)
        for at, span in enumerate(spans)
    ]

    @pl.when(opens)
    def _():
        local_in[...] = jnp.zeros_like(local_in)

        @pl.when(send_local)
        def _():
            local_out[...] = b_half[...].astype(BF16)
            for hop in local_hops:
                hop.start()

    @pl.when(recv_x)
    def _():
        x_hop.wait_recv()

        @pl.when(send_x)
        def _():
            x_step(True)

        for gather in gathers:
            gather.start()
        prefix[own_part, :] = x_in[...]

    @pl.when(recv_local)
    def _():
        for at, span in enumerate(spans):
            local_hops[at].wait_recv()

            @pl.when(send_local)
            def _(at=at, span=span):
                here = local_in[span, :]
                ahead = here.astype(F32) + dot(here, pair[...]) + b_half[span, :]
                local_out[span, :] = ahead.astype(BF16)
                local_hops[at].start()

    @pl.when(recv_x)
    def _():
        landed = prefix.at[pl.ds(0, (columns - 1) * part), :]
        remote(landed, landed, gather_send.at[0], gather_recv, layer=partner).wait_recv()
        swap.start()
        swap.wait_recv()

    def chunk(at):
        return pl.ds(pl.multiple_of(mine + at * step, step), step)

    shares = [
        remote(carried.at[chunk(at), :], carried.at[chunk(at), :], share_send.at[at], share_recv.at[at], layer=partner)
        for at in range(CHUNKS)
    ]
    e_hops = [
        [
            remote(
                e_out.at[span, :], e_in.at[span, :], e_send.at[(away - 1) * CHUNKS + at], e_recv.at[at],
                layer=me + 2 * away,
            )
            for at, span in enumerate(spans)
        ]
        for away in range(1, widest + 1)
    ]

    for at, span in enumerate(spans):
        @pl.when(jnp.logical_not(later))
        def _(at=at, span=span):
            carried[chunk(at), :] = local_in[span, :]
            c_half[span, :] = local_in[span, :].astype(F32)

        @pl.when(later)
        def _(at=at, span=span):
            e_hops[0][at].wait_recv()

            @pl.when(opens)
            def _():
                carried[chunk(at), :] = e_in[span, :]
                c_half[span, :] = e_in[span, :].astype(F32)

            @pl.when(recv_local)
            def _():
                here = e_in[span, :]
                total = local_in[span, :].astype(F32) + here.astype(F32) + dot(here, prefix[...])
                carried[chunk(at), :] = total.astype(BF16)
                c_half[span, :] = total

        shares[at].start()

        @pl.when(send_e)
        def _(at=at, span=span):
            ahead = c_half[span, :] + dot(carried[chunk(at), :], pair[...]) + b_half[span, :]
            e_out[span, :] = ahead.astype(BF16)
            for away in range(1, widest + 1):
                @pl.when(following_size == away)
                def _(away=away):
                    e_hops[away - 1][at].start()

    @pl.when(send_e)
    def _():
        for away in range(widest - 1, 0, -1):
            @pl.when(following_size > away)
            def _(away=away):
                for hop in e_hops[away - 1]:
                    hop.start()

    def finish(offset):
        span = pl.ds(pl.multiple_of(offset, half), half)

        @pl.when(core == 0)
        def _():
            c_ref[span, :] = (states_ref[span, :].astype(F32) + carried[span, :].astype(F32)).astype(BF16)

        @pl.when(core == 1)
        def _():
            here = carried[span, :]
            correction = here.astype(F32) + dot(here, maps[0]) + d_all[span, :]
            c_ref[span, :] = (states_ref[span, :].astype(F32) + correction).astype(BF16)

        f_ref[span, :] = advance(c_ref[span, :], win[0], wout[0])

    finish(mine)
    for share in shares:
        share.wait_recv()
    finish(half - mine)

    share_map.wait_send()
    share_half.wait_send()
    for share in shares:
        share.wait_send()

    @pl.when(me > 0)
    def _():
        to_before.wait_send()

    @pl.when(send_x)
    def _():
        x_hop.wait_send()

    @pl.when(recv_x)
    def _():
        for gather in gathers:
            gather.wait_send()
        swap.wait_send()

    @pl.when(send_local)
    def _():
        for hop in local_hops:
            hop.wait_send()

    @pl.when(send_e)
    def _():
        for away in range(1, widest + 1):
            @pl.when(following_size >= away)
            def _(away=away):
                for hop in e_hops[away - 1]:
                    hop.wait_send()


def shards(layers, columns, states, w_in, w_out):
    rows, width = states.shape[1:]
    hidden = w_in.shape[2]
    half = rows // 2
    part = width // (2 * columns)
    widest = max(groups_of(layers // 2)[1:])
    block = jax.ShapeDtypeStruct((rows, width), BF16)
    vmem = pl.BlockSpec(memory_space=pltpu.VMEM)
    hbm = pl.BlockSpec(memory_space=pl.ANY)
    dma = pltpu.SemaphoreType.DMA
    corrected, fine = pl.pallas_call(
        functools.partial(kernel, layers, columns),
        out_shape=(block, block),
        in_specs=[vmem, hbm, hbm],
        out_specs=(vmem, vmem),
        scratch_shapes=[
            pltpu.VMEM((2, width, hidden), BF16),
            pltpu.VMEM((2, hidden, width), BF16),
            pltpu.VMEM((rows, width), BF16),
            pltpu.VMEM((2, width, width), BF16),
            pltpu.VMEM((width, width), BF16),
            pltpu.VMEM((rows, width), F32),
            pltpu.VMEM((rows, width), BF16),
            pltpu.VMEM((rows, width), BF16),
            pltpu.VMEM((rows, width), F32),
            pltpu.VMEM((half, width), F32),
            pltpu.VMEM((rows, width), BF16),
            pltpu.VMEM((half, width), BF16),
            pltpu.VMEM((half, width), BF16),
            pltpu.VMEM((part, width), BF16),
            pltpu.VMEM((part, width), BF16),
            pltpu.VMEM((width, width), BF16),
            pltpu.VMEM((half, width), BF16),
            pltpu.VMEM((half, width), BF16),
            pltpu.VMEM((half, width), F32),
            dma((4,)),
            dma((2,)),
            dma((2,)),
            dma((2,)),
            dma((2,)),
            dma((columns,)),
            dma,
            dma((2,)),
            dma((CHUNKS,)),
            dma((CHUNKS,)),
            dma((widest * CHUNKS,)),
            dma((CHUNKS,)),
            dma((CHUNKS,)),
            dma((CHUNKS,)),
        ],
        compiler_params=pltpu.CompilerParams(
            collective_id=0, has_side_effects=True, vmem_limit_bytes=67043328
        ),
    )(states[0], w_in, w_out)
    return (corrected[None], fine[None])


def solution(mesh):
    return jax.shard_map(
        functools.partial(shards, mesh.shape["layer"], mesh.shape["dp"]),
        mesh=mesh,
        in_specs=(P("layer", "dp", None), P("layer", None, None), P("layer", None, None)),
        out_specs=(P("layer", "dp", None), P("layer", "dp", None)),
        check_vma=False,
    )
```

```python
import functools

import jax
import jax.numpy as jnp
from jax import lax
from jax.experimental import pallas as pl
from jax.experimental.pallas import tpu as pltpu
from jax.sharding import PartitionSpec as P

F32, BF16 = jnp.float32, jnp.bfloat16
ROOT_HALF = 0.7071067811865476
CHUNKS = 2


def groups_of(chips):
    if chips == 16:
        return (4, 3, 5, 4)
    return (chips // 3, chips // 3, chips - 2 * (chips // 3))


def dot(left, right):
    return jnp.dot(left, right, preferred_element_type=F32)


def gelu(x):
    return 0.5 * x * (1.0 + lax.erf(x * ROOT_HALF))


def advance(state, w_first, w_second):
    gated = gelu(dot(state, w_first)).astype(BF16)
    return (state.astype(F32) + 0.25 * dot(gated, w_second)).astype(BF16)


def kernel(
    layers, columns, states_hbm, win_hbm, wout_hbm, c_hbm, f_hbm,
    state, win, wout, follow, maps, pair, defect, half_out, half_in, d_all, b_half, carried,
    local_in, local_out, x_in, x_out, prefix, jump, base, e_in, e_out, c_buf, f_buf,
    load_sem, follow_sems, map_sems, half_sems, x_sems, gather_send, gather_recv, swap_sems,
    local_send, local_recv, e_send, e_recv, share_send, share_recv, store_sem, hello, plane,
):
    me, column = lax.axis_index("layer"), lax.axis_index("dp")
    core, chip = lax.rem(me, 2), me // 2
    partner = me + 1 - 2 * core
    rows, width = state.shape
    half, half_width = rows // 2, width // 2
    step = half // CHUNKS
    part = half_width // columns
    mine = core * half
    both, neither = jnp.logical_and, jnp.logical_not

    sizes = groups_of(layers // 2)
    widest = max(sizes[1:])
    start, size, following_size, at = 0, sizes[0], sizes[1], 0
    for k in range(1, len(sizes)):
        at += sizes[k - 1]
        reached = (chip >= at).astype(jnp.int32)
        ahead = sizes[k + 1] if k + 1 < len(sizes) else 0
        start = start + reached * sizes[k - 1]
        size = size + reached * (sizes[k] - sizes[k - 1])
        following_size = following_size + reached * (ahead - sizes[k])
    to_close = start + size - 1 - chip
    opens, closes = chip == start, to_close == 0
    later, first, last = chip >= sizes[0], chip == 0, chip == layers // 2 - 1
    recv_local, send_local = neither(opens), neither(closes)
    recv_x, send_x = both(recv_local, later), both(send_local, later)
    send_e = both(closes, following_size > 0)
    send_map, recv_map = me > 0, me != 1

    def number(flag):
        return flag.astype(jnp.int32)

    def remote(source, target, send, recv, **device):
        return pltpu.make_async_remote_copy(
            src_ref=source, dst_ref=target, send_sem=send, recv_sem=recv, device_id=device
        )

    loads = [
        pltpu.make_async_copy(source, target, load_sem.at[slot])
        for slot, (source, target) in enumerate((
            (win_hbm.at[0], win.at[0]),
            (wout_hbm.at[0], wout.at[0]),
            (states_hbm, state),
            (win_hbm.at[1], win.at[1]),
            (wout_hbm.at[1], wout.at[1]),
        ))
    ]
    for load in loads:
        load.start()

    barrier = pltpu.get_barrier_semaphore()
    send_back = both(core == 0, me > 0)
    recv_back = both(core == 1, me < layers - 1)

    def greet(**device):
        pl.semaphore_signal(barrier, inc=1, device_id=device)

    greet(layer=partner)

    @pl.when(recv_back)
    def _():
        greet(layer=me + 1)

    @pl.when(neither(first))
    def _():
        greet(layer=me - 2)

    @pl.when(neither(last))
    def _():
        greet(layer=me + 2)

    side = 4 if columns % 4 == 0 else 1
    depth = columns // side
    line, place = column // depth, lax.rem(column, depth)
    in_line = [line * depth + lax.rem(place + turn, depth) for turn in range(1, depth)]
    across = [lax.rem(line + turn, side) * depth + place for turn in range(1, side)]

    @pl.when(recv_x)
    def _():
        for peer in in_line + across:
            greet(dp=peer)

    loads[0].wait()
    loads[1].wait()
    own_map = maps.at[core]

    @pl.when(send_map)
    def _():
        own_map[...] = (0.25 * dot(win[0], wout[0])).astype(BF16)

    loads[2].wait()
    pl.semaphore_wait(
        barrier,
        1 + number(send_back) + number(neither(first)) + number(neither(last))
        + number(recv_x) * (len(in_line) + len(across)),
    )
    share_map = remote(own_map, own_map, map_sems.at[0], map_sems.at[1], layer=partner)

    @pl.when(send_map)
    def _():
        share_map.start()

    to_before = remote(state, follow, follow_sems.at[0], follow_sems.at[1], layer=me - 1)

    @pl.when(me > 0)
    def _():
        to_before.start()

    @pl.when(recv_x)
    def _():
        for peer in across:
            pl.semaphore_signal(plane, inc=1, device_id={"dp": peer})

    def pass_hello(turn):
        @pl.when(both(to_close == turn, neither(first)))
        def _():
            if turn > 0:
                pl.semaphore_wait(hello, 1)
            pl.semaphore_signal(hello, inc=1, device_id={"layer": me - 2})

    @pl.when(both(first, neither(closes)))
    def _():
        pl.semaphore_wait(hello, 1)

    pass_hello(0)
    relaxed = advance(state[...], win[0], wout[0])
    pass_hello(1)

    loads[3].wait()
    loads[4].wait()
    pushed = advance(relaxed, win[1], wout[1])

    @pl.when(me < layers - 1)
    def _():
        to_before.wait_recv()

    @pl.when(me == layers - 1)
    def _():
        follow[...] = jnp.zeros_like(follow)

    defect[...] = pushed.astype(F32) - follow[...].astype(F32)
    half_out[...] = defect[...].astype(BF16)
    share_half = remote(half_out, half_in, half_sems.at[0], half_sems.at[1], layer=partner)
    share_half.start()
    pass_hello(2)

    @pl.when(recv_map)
    def _():
        share_map.wait_recv()

    @pl.when(neither(first))
    def _():
        even_map, odd_map = maps[0], maps[1]
        pair[...] = (even_map.astype(F32) + odd_map.astype(F32) + dot(even_map, odd_map)).astype(BF16)

    own_part = pl.ds(pl.multiple_of(core * half_width + column * part, part), part)
    x_hop = remote(x_out, x_in, x_sems.at[0], x_sems.at[1], layer=me + 2)
    peers = [lax.rem(column + turn, columns) for turn in range(1, columns)]
    gathers = [
        remote(x_in, prefix.at[own_part, :], gather_send.at[turn], gather_recv, dp=peer)
        for turn, peer in enumerate(peers)
    ]
    half_prefix = prefix.at[pl.ds(pl.multiple_of(core * half_width, half_width), half_width), :]
    swap = remote(half_prefix, half_prefix, swap_sems.at[0], swap_sems.at[1], layer=partner)

    @pl.when(both(send_x, opens))
    def _():
        x_out[...] = pair[own_part, :]
        x_hop.start()

    pass_hello(3)
    share_half.wait_recv()
    own_rows = pl.ds(pl.multiple_of(mine, half), half)

    @pl.when(core == 0)
    def _():
        d_all[...] = defect[...]
        b_half[...] = half_in[own_rows, :].astype(F32)

    @pl.when(core == 1)
    def _():
        d_all[...] = half_in[...].astype(F32)
        b_half[...] = defect[own_rows, :]

    even_half = d_all[own_rows, :]
    b_half[...] += even_half + dot(even_half.astype(BF16), maps[1])

    spans = [pl.ds(at * step, step) for at in range(CHUNKS)]
    local_hops = [
        remote(local_out.at[span, :], local_in.at[span, :], local_send.at[at], local_recv.at[at], layer=me + 2)
        for at, span in enumerate(spans)
    ]
    e_hops = [
        [
            remote(
                e_out.at[span, :], e_in.at[span, :], e_send.at[(away - 1) * CHUNKS + at], e_recv.at[at],
                layer=me + 2 * away,
            )
            for at, span in enumerate(spans)
        ]
        for away in range(1, widest + 1)
    ]

    def send_far(at):
        for away in range(1, widest + 1):
            @pl.when(following_size == away)
            def _(away=away):
                e_hops[away - 1][at].start()

    def send_others():
        for away in range(widest - 1, 0, -1):
            @pl.when(following_size > away)
            def _(away=away):
                for hop in e_hops[away - 1]:
                    hop.start()

    @pl.when(opens)
    def _():
        local_out[...] = b_half[...].astype(BF16)
        for hop in local_hops:
            hop.start()

    pass_hello(4)

    @pl.when(recv_x)
    def _():
        x_hop.wait_recv()

        @pl.when(send_x)
        def _():
            x = x_in[...]
            x_out[...] = (pair[own_part, :].astype(F32) + x.astype(F32) + dot(x, pair[...])).astype(BF16)
            x_hop.start()

        if across:
            pl.semaphore_wait(plane, len(across))
        for gather in gathers:
            gather.start()
        prefix[own_part, :] = x_in[...]

    @pl.when(send_e)
    def _():
        pl.semaphore_wait(hello, 1)

    @pl.when(recv_local)
    def _():
        for at, span in enumerate(spans):
            local_hops[at].wait_recv()

            @pl.when(neither(last))
            def _(at=at, span=span):
                here = local_in[span, :]
                ahead = here.astype(F32) + dot(here, pair[...]) + b_half[span, :]

                @pl.when(send_local)
                def _():
                    local_out[span, :] = ahead.astype(BF16)
                    local_hops[at].start()

                @pl.when(both(closes, later))
                def _():
                    base[span, :] = ahead

                @pl.when(both(closes, neither(later)))
                def _():
                    e_out[span, :] = ahead.astype(BF16)
                    send_far(at)

    @pl.when(both(closes, neither(later)))
    def _():
        send_others()

    @pl.when(recv_x)
    def _():
        landed = prefix.at[pl.ds(0, (columns - 1) * part), :]
        remote(landed, landed, gather_send.at[0], gather_recv, layer=partner).wait_recv()
        swap.start()
        swap.wait_recv()

        @pl.when(send_e)
        def _():
            whole = prefix[...]
            jump[...] = (whole.astype(F32) + pair[...].astype(F32) + dot(whole, pair[...])).astype(BF16)

    def chunk(at):
        return pl.ds(pl.multiple_of(mine + at * step, step), step)

    shares = [
        remote(carried.at[chunk(at), :], carried.at[chunk(at), :], share_send.at[at], share_recv.at[at], layer=partner)
        for at in range(CHUNKS)
    ]

    @pl.when(first)
    def _():
        carried[...] = jnp.zeros_like(carried)

    @pl.when(both(neither(later), neither(first)))
    def _():
        for at, span in enumerate(spans):
            carried[chunk(at), :] = local_in[span, :]
            shares[at].start()

    def with_entering(at, span):
        here = e_in[span, :]

        @pl.when(opens)
        def _():
            carried[chunk(at), :] = here

        @pl.when(recv_local)
        def _():
            total = local_in[span, :].astype(F32) + here.astype(F32) + dot(here, prefix[...])
            carried[chunk(at), :] = total.astype(BF16)

        shares[at].start()

    @pl.when(both(later, send_e))
    def _():
        for at, span in enumerate(spans):
            e_hops[0][at].wait_recv()
            here = e_in[span, :]
            ahead = base[span, :] + here.astype(F32) + dot(here, jump[...])
            e_out[span, :] = ahead.astype(BF16)
            send_far(at)
        send_others()
        for at, span in enumerate(spans):
            with_entering(at, span)

    @pl.when(both(later, neither(send_e)))
    def _():
        for at, span in enumerate(spans):
            e_hops[0][at].wait_recv()
            with_entering(at, span)

    stores = []

    def finish(offset, slot):
        span = pl.ds(pl.multiple_of(offset, half), half)

        @pl.when(core == 0)
        def _():
            c_buf[span, :] = (state[span, :].astype(F32) + carried[span, :].astype(F32)).astype(BF16)

        @pl.when(both(core == 1, neither(first)))
        def _():
            here = carried[span, :]
            correction = here.astype(F32) + dot(here, maps[0]) + d_all[span, :]
            c_buf[span, :] = (state[span, :].astype(F32) + correction).astype(BF16)

        @pl.when(both(core == 1, first))
        def _():
            c_buf[span, :] = (state[span, :].astype(F32) + d_all[span, :]).astype(BF16)

        for buffer, out, at in ((c_buf, c_hbm, 0), (f_buf, f_hbm, 1)):
            stores.append(pltpu.make_async_copy(buffer.at[span, :], out.at[span, :], store_sem.at[2 * slot + at]))
        stores[-2].start()
        f_buf[span, :] = advance(c_buf[span, :], win[0], wout[0])
        stores[-1].start()

    finish(mine, 0)

    @pl.when(neither(first))
    def _():
        for share in shares:
            share.wait_recv()

    finish(half - mine, 1)
    share_half.wait_send()

    @pl.when(neither(first))
    def _():
        for share in shares:
            share.wait_send()

    @pl.when(send_map)
    def _():
        share_map.wait_send()
        to_before.wait_send()

    @pl.when(send_x)
    def _():
        x_hop.wait_send()

    @pl.when(recv_x)
    def _():
        for gather in gathers:
            gather.wait_send()
        swap.wait_send()

    @pl.when(send_local)
    def _():
        for hop in local_hops:
            hop.wait_send()

    @pl.when(send_e)
    def _():
        for away in range(1, widest + 1):
            @pl.when(following_size >= away)
            def _(away=away):
                for hop in e_hops[away - 1]:
                    hop.wait_send()

    for store in stores:
        store.wait()


def shards(layers, columns, states, w_in, w_out):
    rows, width = states.shape[1:]
    hidden = w_in.shape[2]
    half = rows // 2
    part = width // (2 * columns)
    widest = max(groups_of(layers // 2)[1:])
    block = jax.ShapeDtypeStruct((rows, width), BF16)
    hbm = pl.BlockSpec(memory_space=pl.ANY)
    dma, vmem = pltpu.SemaphoreType.DMA, pltpu.VMEM
    corrected, fine = pl.pallas_call(
        functools.partial(kernel, layers, columns),
        out_shape=(block, block),
        in_specs=[hbm, hbm, hbm],
        out_specs=(hbm, hbm),
        scratch_shapes=[
            vmem((rows, width), BF16),
            vmem((2, width, hidden), BF16),
            vmem((2, hidden, width), BF16),
            vmem((rows, width), BF16),
            vmem((2, width, width), BF16),
            vmem((width, width), BF16),
            vmem((rows, width), F32),
            vmem((rows, width), BF16),
            vmem((rows, width), BF16),
            vmem((rows, width), F32),
            vmem((half, width), F32),
            vmem((rows, width), BF16),
            vmem((half, width), BF16),
            vmem((half, width), BF16),
            vmem((part, width), BF16),
            vmem((part, width), BF16),
            vmem((width, width), BF16),
            vmem((width, width), BF16),
            vmem((half, width), F32),
            vmem((half, width), BF16),
            vmem((half, width), BF16),
            vmem((rows, width), BF16),
            vmem((rows, width), BF16),
            dma((5,)),
            dma((2,)),
            dma((2,)),
            dma((2,)),
            dma((2,)),
            dma((columns,)),
            dma,
            dma((2,)),
            dma((CHUNKS,)),
            dma((CHUNKS,)),
            dma((widest * CHUNKS,)),
            dma((CHUNKS,)),
            dma((CHUNKS,)),
            dma((CHUNKS,)),
            dma((4,)),
            pltpu.SemaphoreType.REGULAR,
            pltpu.SemaphoreType.REGULAR,
        ],
        compiler_params=pltpu.CompilerParams(
            collective_id=0, has_side_effects=True, vmem_limit_bytes=67043328
        ),
    )(states[0], w_in, w_out)
    return (corrected[None], fine[None])


def solution(mesh):
    return jax.shard_map(
        functools.partial(shards, mesh.shape["layer"], mesh.shape["dp"]),
        mesh=mesh,
        in_specs=(P("layer", "dp", None), P("layer", None, None), P("layer", None, None)),
        out_specs=(P("layer", "dp", None), P("layer", "dp", None)),
        check_vma=False,
    )
```

```python
import functools

import jax
import jax.numpy as jnp
from jax import lax
from jax.experimental import pallas as pl
from jax.experimental.pallas import tpu as pltpu
from jax.sharding import PartitionSpec as P

F32, BF16 = jnp.float32, jnp.bfloat16
ROOT_HALF = 0.7071067811865476
CHUNKS = 2


def groups_of(chips):
    if chips == 16:
        return (4, 4, 5, 3)
    return (chips // 3, chips // 3, chips - 2 * (chips // 3))


def dot(left, right):
    return jnp.dot(left, right, preferred_element_type=F32)


def gelu(x):
    return 0.5 * x * (1.0 + lax.erf(x * ROOT_HALF))


def advance(state, w_first, w_second):
    gated = gelu(dot(state, w_first)).astype(BF16)
    return (state.astype(F32) + 0.25 * dot(gated, w_second)).astype(BF16)


def kernel(
    layers, columns, states_hbm, win_hbm, wout_hbm, both_hbm,
    state, win, wout, follow, maps, pair, defect, half_out, half_in, d_all, b_half, carried,
    local_in, local_out, x_in, x_out, prefix, jump, base, e_in, e_out, c_buf, f_buf,
    load_sem, follow_sems, map_sems, half_sems, x_sems, gather_send, gather_recv, swap_sems,
    local_send, local_recv, e_send, e_recv, share_send, share_recv, store_sem, hello, plane,
):
    me, column = lax.axis_index("layer"), lax.axis_index("dp")
    core, chip = lax.rem(me, 2), me // 2
    partner = me + 1 - 2 * core
    rows, width = state.shape
    half, half_width = rows // 2, width // 2
    step = half // CHUNKS
    part = half_width // columns
    mine = core * half
    both, neither = jnp.logical_and, jnp.logical_not

    sizes = groups_of(layers // 2)
    widest = max(sizes[1:])
    start, size, following_size, at = 0, sizes[0], sizes[1], 0
    for k in range(1, len(sizes)):
        at += sizes[k - 1]
        reached = (chip >= at).astype(jnp.int32)
        ahead = sizes[k + 1] if k + 1 < len(sizes) else 0
        start = start + reached * sizes[k - 1]
        size = size + reached * (sizes[k] - sizes[k - 1])
        following_size = following_size + reached * (ahead - sizes[k])
    to_close = start + size - 1 - chip
    opens, closes = chip == start, to_close == 0
    later, first, last = chip >= sizes[0], chip == 0, chip == layers // 2 - 1
    recv_local, send_local = neither(opens), neither(closes)
    recv_x, send_x = both(recv_local, later), both(send_local, later)
    send_e = both(closes, following_size > 0)
    send_map, recv_map = me > 0, me != 1

    def number(flag):
        return flag.astype(jnp.int32)

    def remote(source, target, send, recv, **device):
        return pltpu.make_async_remote_copy(
            src_ref=source, dst_ref=target, send_sem=send, recv_sem=recv, device_id=device
        )

    loads = [
        pltpu.make_async_copy(source, target, load_sem.at[slot])
        for slot, (source, target) in enumerate((
            (states_hbm, state),
            (win_hbm.at[0], win.at[0]),
            (wout_hbm.at[0], wout.at[0]),
            (win_hbm.at[1], win.at[1]),
            (wout_hbm.at[1], wout.at[1]),
        ))
    ]
    for load in loads[:3]:
        load.start()

    barrier = pltpu.get_barrier_semaphore()
    send_back = both(core == 0, me > 0)
    recv_back = both(core == 1, me < layers - 1)

    def greet(**device):
        pl.semaphore_signal(barrier, inc=1, device_id=device)

    greet(layer=partner)

    @pl.when(recv_back)
    def _():
        greet(layer=me + 1)

    @pl.when(neither(first))
    def _():
        greet(layer=me - 2)

    @pl.when(neither(last))
    def _():
        greet(layer=me + 2)

    side = 4 if columns % 4 == 0 else 1
    depth = columns // side
    line, place = column // depth, lax.rem(column, depth)
    in_line = [line * depth + lax.rem(place + turn, depth) for turn in range(1, depth)]
    across = [lax.rem(line + turn, side) * depth + place for turn in range(1, side)]

    @pl.when(recv_x)
    def _():
        for peer in in_line + across:
            greet(dp=peer)

    loads[0].wait()
    for load in loads[3:]:
        load.start()
    loads[1].wait()
    loads[2].wait()
    own_map = maps.at[core]

    @pl.when(send_map)
    def _():
        own_map[...] = (0.25 * dot(win[0], wout[0])).astype(BF16)

    pl.semaphore_wait(
        barrier,
        1 + number(send_back) + number(neither(first)) + number(neither(last))
        + number(recv_x) * (len(in_line) + len(across)),
    )
    share_map = remote(own_map, own_map, map_sems.at[0], map_sems.at[1], layer=partner)

    @pl.when(send_map)
    def _():
        share_map.start()

    to_before = remote(state, follow, follow_sems.at[0], follow_sems.at[1], layer=me - 1)

    @pl.when(me > 0)
    def _():
        to_before.start()

    @pl.when(recv_x)
    def _():
        for peer in across:
            pl.semaphore_signal(plane, inc=1, device_id={"dp": peer})

    def pass_hello(turn):
        @pl.when(both(to_close == turn, later))
        def _():
            if turn > 0:
                pl.semaphore_wait(hello, 1)
            pl.semaphore_signal(hello, inc=1, device_id={"layer": me - 2})

    pass_hello(0)
    relaxed = advance(state[...], win[0], wout[0])
    pass_hello(1)

    loads[3].wait()
    loads[4].wait()
    pushed = advance(relaxed, win[1], wout[1])

    @pl.when(me < layers - 1)
    def _():
        to_before.wait_recv()

    @pl.when(me == layers - 1)
    def _():
        follow[...] = jnp.zeros_like(follow)

    defect[...] = pushed.astype(F32) - follow[...].astype(F32)
    half_out[...] = defect[...].astype(BF16)
    share_half = remote(half_out, half_in, half_sems.at[0], half_sems.at[1], layer=partner)
    share_half.start()
    pass_hello(2)

    @pl.when(recv_map)
    def _():
        share_map.wait_recv()

    @pl.when(neither(first))
    def _():
        even_map, odd_map = maps[0], maps[1]
        pair[...] = (even_map.astype(F32) + odd_map.astype(F32) + dot(even_map, odd_map)).astype(BF16)

    own_part = pl.ds(pl.multiple_of(core * half_width + column * part, part), part)
    x_hop = remote(x_out, x_in, x_sems.at[0], x_sems.at[1], layer=me + 2)
    peers = [lax.rem(column + turn, columns) for turn in range(1, columns)]
    gathers = [
        remote(x_in, prefix.at[own_part, :], gather_send.at[turn], gather_recv, dp=peer)
        for turn, peer in enumerate(peers)
    ]
    half_prefix = prefix.at[pl.ds(pl.multiple_of(core * half_width, half_width), half_width), :]
    swap = remote(half_prefix, half_prefix, swap_sems.at[0], swap_sems.at[1], layer=partner)

    @pl.when(both(send_x, opens))
    def _():
        x_out[...] = pair[own_part, :]
        x_hop.start()

    pass_hello(3)
    share_half.wait_recv()
    own_rows = pl.ds(pl.multiple_of(mine, half), half)

    @pl.when(core == 0)
    def _():
        d_all[...] = defect[...]
        b_half[...] = half_in[own_rows, :].astype(F32)

    @pl.when(core == 1)
    def _():
        d_all[...] = half_in[...].astype(F32)
        b_half[...] = defect[own_rows, :]

    even_half = d_all[own_rows, :]
    b_half[...] += even_half + dot(even_half.astype(BF16), maps[1])

    spans = [pl.ds(at * step, step) for at in range(CHUNKS)]
    local_hops = [
        remote(local_out.at[span, :], local_in.at[span, :], local_send.at[at], local_recv.at[at], layer=me + 2)
        for at, span in enumerate(spans)
    ]
    e_hops = [
        [
            remote(
                e_out.at[span, :], e_in.at[span, :], e_send.at[(away - 1) * CHUNKS + at], e_recv.at[at],
                layer=me + 2 * away,
            )
            for at, span in enumerate(spans)
        ]
        for away in range(1, widest + 1)
    ]

    def send_far(at):
        for away in range(1, widest + 1):
            @pl.when(following_size == away)
            def _(away=away):
                e_hops[away - 1][at].start()

    def send_others():
        for away in range(widest - 1, 0, -1):
            @pl.when(following_size > away)
            def _(away=away):
                for hop in e_hops[away - 1]:
                    hop.start()

    @pl.when(opens)
    def _():
        local_out[...] = b_half[...].astype(BF16)
        for hop in local_hops:
            hop.start()

    for turn in range(4, max(sizes)):
        pass_hello(turn)

    @pl.when(recv_x)
    def _():
        x_hop.wait_recv()

        @pl.when(send_x)
        def _():
            x = x_in[...]
            x_out[...] = (pair[own_part, :].astype(F32) + x.astype(F32) + dot(x, pair[...])).astype(BF16)
            x_hop.start()

        if across:
            pl.semaphore_wait(plane, len(across))
        for gather in gathers:
            gather.start()
        prefix[own_part, :] = x_in[...]

    @pl.when(send_e)
    def _():
        pl.semaphore_wait(hello, 1)

    @pl.when(recv_local)
    def _():
        for at, span in enumerate(spans):
            local_hops[at].wait_recv()

            @pl.when(neither(last))
            def _(at=at, span=span):
                here = local_in[span, :]
                ahead = here.astype(F32) + dot(here, pair[...]) + b_half[span, :]

                @pl.when(send_local)
                def _():
                    local_out[span, :] = ahead.astype(BF16)
                    local_hops[at].start()

                @pl.when(both(closes, later))
                def _():
                    base[span, :] = ahead

                @pl.when(both(closes, neither(later)))
                def _():
                    e_out[span, :] = ahead.astype(BF16)
                    send_far(at)

    @pl.when(recv_x)
    def _():
        landed = prefix.at[pl.ds(0, (columns - 1) * part), :]
        remote(landed, landed, gather_send.at[0], gather_recv, layer=partner).wait_recv()
        swap.start()
        swap.wait_recv()

        @pl.when(send_e)
        def _():
            whole = prefix[...]
            jump[...] = (whole.astype(F32) + pair[...].astype(F32) + dot(whole, pair[...])).astype(BF16)

    def chunk(at):
        return pl.ds(pl.multiple_of(mine + at * step, step), step)

    shares = [
        remote(carried.at[chunk(at), :], carried.at[chunk(at), :], share_send.at[at], share_recv.at[at], layer=partner)
        for at in range(CHUNKS)
    ]

    @pl.when(first)
    def _():
        carried[...] = jnp.zeros_like(carried)

    @pl.when(both(neither(later), neither(first)))
    def _():
        for at, span in enumerate(spans):
            carried[chunk(at), :] = local_in[span, :]
            shares[at].start()

    def with_entering(at, span):
        here = e_in[span, :]

        @pl.when(opens)
        def _():
            carried[chunk(at), :] = here

        @pl.when(recv_local)
        def _():
            total = local_in[span, :].astype(F32) + here.astype(F32) + dot(here, prefix[...])
            carried[chunk(at), :] = total.astype(BF16)

        shares[at].start()

    @pl.when(both(later, send_e))
    def _():
        for at, span in enumerate(spans):
            e_hops[0][at].wait_recv()
            here = e_in[span, :]
            ahead = base[span, :] + here.astype(F32) + dot(here, jump[...])
            e_out[span, :] = ahead.astype(BF16)
            send_far(at)
        send_others()
        for at, span in enumerate(spans):
            with_entering(at, span)

    @pl.when(both(later, neither(send_e)))
    def _():
        for at, span in enumerate(spans):
            e_hops[0][at].wait_recv()
            with_entering(at, span)

    stores = []

    def finish(offset, slot):
        span = pl.ds(pl.multiple_of(offset, half), half)

        @pl.when(core == 0)
        def _():
            c_buf[span, :] = (state[span, :].astype(F32) + carried[span, :].astype(F32)).astype(BF16)

        @pl.when(both(core == 1, neither(first)))
        def _():
            here = carried[span, :]
            correction = here.astype(F32) + dot(here, maps[0]) + d_all[span, :]
            c_buf[span, :] = (state[span, :].astype(F32) + correction).astype(BF16)

        @pl.when(both(core == 1, first))
        def _():
            c_buf[span, :] = (state[span, :].astype(F32) + d_all[span, :]).astype(BF16)

        for buffer, out, at in ((c_buf, both_hbm.at[0], 0), (f_buf, both_hbm.at[1], 1)):
            stores.append(pltpu.make_async_copy(buffer.at[span, :], out.at[span, :], store_sem.at[2 * slot + at]))
        stores[-2].start()
        f_buf[span, :] = advance(c_buf[span, :], win[0], wout[0])
        stores[-1].start()

    finish(mine, 0)

    @pl.when(both(closes, neither(later)))
    def _():
        send_others()

    @pl.when(neither(first))
    def _():
        for share in shares:
            share.wait_recv()

    finish(half - mine, 1)
    share_half.wait_send()

    @pl.when(neither(first))
    def _():
        for share in shares:
            share.wait_send()

    @pl.when(send_map)
    def _():
        share_map.wait_send()
        to_before.wait_send()

    @pl.when(send_x)
    def _():
        x_hop.wait_send()

    @pl.when(recv_x)
    def _():
        for gather in gathers:
            gather.wait_send()
        swap.wait_send()

    @pl.when(send_local)
    def _():
        for hop in local_hops:
            hop.wait_send()

    @pl.when(send_e)
    def _():
        for away in range(1, widest + 1):
            @pl.when(following_size >= away)
            def _(away=away):
                for hop in e_hops[away - 1]:
                    hop.wait_send()

    for store in stores:
        store.wait()


def shards(layers, columns, states, w_in, w_out):
    rows, width = states.shape[1:]
    hidden = w_in.shape[2]
    half = rows // 2
    part = width // (2 * columns)
    widest = max(groups_of(layers // 2)[1:])
    block = jax.ShapeDtypeStruct((rows, width), BF16)
    hbm = pl.BlockSpec(memory_space=pl.ANY)
    dma, vmem = pltpu.SemaphoreType.DMA, pltpu.VMEM
    result = pl.pallas_call(
        functools.partial(kernel, layers, columns),
        out_shape=jax.ShapeDtypeStruct((2, rows, width), BF16),
        in_specs=[hbm, hbm, hbm],
        out_specs=hbm,
        scratch_shapes=[
            vmem((rows, width), BF16),
            vmem((2, width, hidden), BF16),
            vmem((2, hidden, width), BF16),
            vmem((rows, width), BF16),
            vmem((2, width, width), BF16),
            vmem((width, width), BF16),
            vmem((rows, width), F32),
            vmem((rows, width), BF16),
            vmem((rows, width), BF16),
            vmem((rows, width), F32),
            vmem((half, width), F32),
            vmem((rows, width), BF16),
            vmem((half, width), BF16),
            vmem((half, width), BF16),
            vmem((part, width), BF16),
            vmem((part, width), BF16),
            vmem((width, width), BF16),
            vmem((width, width), BF16),
            vmem((half, width), F32),
            vmem((half, width), BF16),
            vmem((half, width), BF16),
            vmem((rows, width), BF16),
            vmem((rows, width), BF16),
            dma((5,)),
            dma((2,)),
            dma((2,)),
            dma((2,)),
            dma((2,)),
            dma((columns,)),
            dma,
            dma((2,)),
            dma((CHUNKS,)),
            dma((CHUNKS,)),
            dma((widest * CHUNKS,)),
            dma((CHUNKS,)),
            dma((CHUNKS,)),
            dma((CHUNKS,)),
            dma((4,)),
            pltpu.SemaphoreType.REGULAR,
            pltpu.SemaphoreType.REGULAR,
        ],
        compiler_params=pltpu.CompilerParams(
            collective_id=0, has_side_effects=True, vmem_limit_bytes=67043328
        ),
    )(states[0], w_in, w_out)
    return (result[0:1], result[1:2])


def solution(mesh):
    return jax.shard_map(
        functools.partial(shards, mesh.shape["layer"], mesh.shape["dp"]),
        mesh=mesh,
        in_specs=(P("layer", "dp", None), P("layer", None, None), P("layer", None, None)),
        out_specs=(P("layer", "dp", None), P("layer", "dp", None)),
        check_vma=False,
    )
```

```python
import functools

import jax
import jax.numpy as jnp
from jax import lax
from jax.experimental import pallas as pl
from jax.experimental.pallas import tpu as pltpu
from jax.sharding import PartitionSpec as P

F32, BF16 = jnp.float32, jnp.bfloat16
ROOT_HALF = 0.7071067811865476
CHUNKS = 2


def groups_of(chips):
    if chips == 16:
        return (4, 4, 5, 3)
    return (chips // 3, chips // 3, chips - 2 * (chips // 3))


def dot(left, right):
    return jnp.dot(left, right, preferred_element_type=F32)


def gelu(x):
    return 0.5 * x * (1.0 + lax.erf(x * ROOT_HALF))


def advance(state, w_first, w_second):
    gated = gelu(dot(state, w_first)).astype(BF16)
    return (state.astype(F32) + 0.25 * dot(gated, w_second)).astype(BF16)


def kernel(
    layers, columns, states_hbm, win_hbm, wout_hbm, both_hbm,
    state, win, wout, follow, maps, pair, pushed, defect, half_out, half_in, d_all, b_half, carried,
    local_in, local_out, x_in, x_out, prefix, jump, base, e_in, e_out, c_buf, f_buf,
    load_sem, follow_send, follow_recv, map_send, map_recv, half_send, half_recv, x_sems, gather_send, gather_recv, swap_sems,
    local_send, local_recv, e_send, e_recv, share_send, share_recv, store_sem, hello, plane, in_plane,
):
    me, column = lax.axis_index("layer"), lax.axis_index("dp")
    core, chip = lax.rem(me, 2), me // 2
    partner = me + 1 - 2 * core
    rows, width = state.shape
    half, half_width = rows // 2, width // 2
    step = half // CHUNKS
    part = half_width // columns
    mine = core * half
    both, neither = jnp.logical_and, jnp.logical_not

    sizes = groups_of(layers // 2)
    widest = max(sizes[1:])
    start, size, following_size, at = 0, sizes[0], sizes[1], 0
    for k in range(1, len(sizes)):
        at += sizes[k - 1]
        reached = (chip >= at).astype(jnp.int32)
        ahead = sizes[k + 1] if k + 1 < len(sizes) else 0
        start = start + reached * sizes[k - 1]
        size = size + reached * (sizes[k] - sizes[k - 1])
        following_size = following_size + reached * (ahead - sizes[k])
    to_close = start + size - 1 - chip
    opens, closes = chip == start, to_close == 0
    later, first, last = chip >= sizes[0], chip == 0, chip == layers // 2 - 1
    recv_local, send_local = neither(opens), neither(closes)
    recv_x, send_x = both(recv_local, later), both(send_local, later)
    send_e = both(closes, following_size > 0)
    send_map, recv_map = me > 0, me != 1
    gate = both(closes, later)

    def number(flag):
        return flag.astype(jnp.int32)

    def remote(source, target, send, recv, **device):
        return pltpu.make_async_remote_copy(
            src_ref=source, dst_ref=target, send_sem=send, recv_sem=recv, device_id=device
        )

    loads = [
        pltpu.make_async_copy(source, target, load_sem.at[slot])
        for slot, (source, target) in enumerate((
            (states_hbm, state),
            (win_hbm.at[0], win.at[0]),
            (wout_hbm.at[0], wout.at[0]),
            (win_hbm.at[1], win.at[1]),
            (wout_hbm.at[1], wout.at[1]),
        ))
    ]
    for load in loads[:3]:
        load.start()

    barrier = pltpu.get_barrier_semaphore()
    send_back = both(core == 0, me > 0)
    recv_back = both(core == 1, me < layers - 1)

    def greet(**device):
        pl.semaphore_signal(barrier, inc=1, device_id=device)

    greet(layer=partner)

    @pl.when(recv_back)
    def _():
        greet(layer=me + 1)

    @pl.when(recv_local)
    def _():
        greet(layer=me - 2)

    @pl.when(both(later, neither(closes)))
    def _():
        greet(layer=me + 2 * to_close)

    @pl.when(send_e)
    def _():
        greet(layer=me + 2 * following_size)

    side = 4 if columns % 4 == 0 else 1
    depth = columns // side
    line, place = column // depth, lax.rem(column, depth)
    in_line = [line * depth + lax.rem(place + turn, depth) for turn in range(1, depth)]
    across = [lax.rem(line + turn, side) * depth + place for turn in range(1, side)]

    @pl.when(gate)
    def _():
        for peer in in_line + across:
            greet(dp=peer)

    loads[0].wait()
    for load in loads[3:]:
        load.start()
    low, high = pl.ds(0, half_width), pl.ds(half_width, half_width)

    def make_map(span):
        maps[core, span, :] = (0.25 * dot(win[0, span, :], wout[0])).astype(BF16)

    @pl.when(gate)
    def _():
        loads[1].wait()
        loads[2].wait()
        make_map(low)
        make_map(high)

    pl.semaphore_wait(
        barrier,
        1 + number(send_back) + number(send_local) + number(gate) * (size + len(in_line) + len(across)),
    )

    def half_at(offset):
        return pl.ds(pl.multiple_of(offset, half), half)

    own_rows, other_rows = half_at(mine), half_at(half - mine)
    to_before = [
        remote(state.at[span, :], follow.at[span, :], follow_send.at[at], follow_recv.at[at], layer=me - 1)
        for at, span in enumerate((own_rows, other_rows))
    ]

    map_hops = [
        remote(maps.at[core, span, :], maps.at[core, span, :], map_send.at[at], map_recv.at[at], layer=partner)
        for at, span in enumerate((low, high))
    ]

    @pl.when(gate)
    def _():
        for hop in map_hops:
            hop.start()

    @pl.when(me > 0)
    def _():
        for copy in to_before:
            copy.start()

    @pl.when(neither(gate))
    def _():
        loads[1].wait()
        loads[2].wait()

        @pl.when(send_map)
        def _():
            for span, hop in zip((low, high), map_hops):
                make_map(span)
                hop.start()

    @pl.when(gate)
    def _():
        pl.semaphore_signal(hello, inc=1, device_id={"layer": 2 * (start - 1) + core})
        for peer in in_line:
            pl.semaphore_signal(in_plane, inc=1, device_id={"dp": peer})

    relaxed = advance(state[...], win[0], wout[0])

    loads[3].wait()
    loads[4].wait()
    pushed[...] = advance(relaxed, win[1], wout[1])
    share_other, share_own = [
        remote(half_out.at[span, :], half_in.at[span, :], half_send.at[at], half_recv.at[at], layer=partner)
        for at, span in enumerate((other_rows, own_rows))
    ]

    @pl.when(me == layers - 1)
    def _():
        follow[...] = jnp.zeros_like(follow)

    def take_defect(at, span):
        @pl.when(me < layers - 1)
        def _():
            to_before[at].wait_recv()

        defect[span, :] = pushed[span, :].astype(F32) - follow[span, :].astype(F32)
        half_out[span, :] = defect[span, :].astype(BF16)

    take_defect(0, other_rows)
    share_other.start()
    take_defect(1, own_rows)

    @pl.when(core == 0)
    def _():
        share_own.start()

    @pl.when(gate)
    def _():
        if in_line:
            pl.semaphore_wait(in_plane, len(in_line))
        for peer in across:
            pl.semaphore_signal(plane, inc=1, device_id={"dp": peer})

    @pl.when(recv_map)
    def _():
        for hop in map_hops:
            hop.wait_recv()

    def pair_rows(span):
        ahead = maps[0, span, :].astype(F32) + maps[1, span, :].astype(F32)
        return (ahead + dot(maps[0, span, :], maps[1])).astype(BF16)

    own_part = pl.ds(pl.multiple_of(core * half_width + column * part, part), part)
    x_hop = remote(x_out, x_in, x_sems.at[0], x_sems.at[1], layer=me + 2)
    peers = [lax.rem(column + turn, columns) for turn in range(1, columns)]
    gathers = [
        remote(x_in, prefix.at[own_part, :], gather_send.at[turn], gather_recv, dp=peer)
        for turn, peer in enumerate(peers)
    ]
    half_prefix = prefix.at[pl.ds(pl.multiple_of(core * half_width, half_width), half_width), :]
    swap = remote(half_prefix, half_prefix, swap_sems.at[0], swap_sems.at[1], layer=partner)

    @pl.when(both(send_x, opens))
    def _():
        x_out[...] = pair_rows(own_part)
        x_hop.start()

    @pl.when(neither(first))
    def _():
        pair[...] = pair_rows(pl.ds(0, width))

    @pl.when(gate)
    def _():
        if across:
            pl.semaphore_wait(plane, len(across))
        for turn in range(1, widest - 1):
            @pl.when(turn < size - 1)
            def _(turn=turn):
                pl.semaphore_signal(plane, inc=1, device_id={"layer": me - 2 * turn})

    @pl.when(recv_x)
    def _():
        x_hop.wait_recv()

        @pl.when(send_x)
        def _():
            x = x_in[...]
            x_out[...] = (pair[own_part, :].astype(F32) + x.astype(F32) + dot(x, pair[...])).astype(BF16)
            x_hop.start()

        @pl.when(send_x)
        def _():
            pl.semaphore_wait(plane, 1)

        for gather in gathers:
            gather.start()
        prefix[own_part, :] = x_in[...]

    share_other.wait_recv()

    @pl.when(core == 0)
    def _():
        d_all[own_rows, :] = defect[own_rows, :]
        b_half[...] = half_in[own_rows, :].astype(F32)

    @pl.when(core == 1)
    def _():
        d_all[own_rows, :] = half_in[own_rows, :].astype(F32)
        b_half[...] = defect[own_rows, :]

    even_half = d_all[own_rows, :]
    b_half[...] += even_half + dot(even_half.astype(BF16), maps[1])

    spans = [pl.ds(at * step, step) for at in range(CHUNKS)]
    local_hops = [
        remote(local_out.at[span, :], local_in.at[span, :], local_send.at[at], local_recv.at[at], layer=me + 2)
        for at, span in enumerate(spans)
    ]
    e_hops = [
        [
            remote(
                e_out.at[span, :], e_in.at[span, :], e_send.at[(away - 1) * CHUNKS + at], e_recv.at[at],
                layer=me + 2 * away,
            )
            for at, span in enumerate(spans)
        ]
        for away in range(1, widest + 1)
    ]

    def send_far(at):
        for away in range(1, widest + 1):
            @pl.when(following_size == away)
            def _(away=away):
                e_hops[away - 1][at].start()

    def send_others():
        for away in range(widest - 1, 0, -1):
            @pl.when(following_size > away)
            def _(away=away):
                for hop in e_hops[away - 1]:
                    hop.start()

    @pl.when(both(opens, send_local))
    def _():
        local_out[...] = b_half[...].astype(BF16)
        for hop in local_hops:
            hop.start()

    @pl.when(send_e)
    def _():
        pl.semaphore_wait(hello, 1)

    @pl.when(recv_local)
    def _():
        for at, span in enumerate(spans):
            local_hops[at].wait_recv()

            @pl.when(neither(last))
            def _(at=at, span=span):
                here = local_in[span, :]
                ahead = here.astype(F32) + dot(here, pair[...]) + b_half[span, :]

                @pl.when(send_local)
                def _():
                    local_out[span, :] = ahead.astype(BF16)
                    local_hops[at].start()

                @pl.when(both(closes, later))
                def _():
                    base[span, :] = ahead

                @pl.when(both(closes, neither(later)))
                def _():
                    e_out[span, :] = ahead.astype(BF16)
                    send_far(at)

    @pl.when(recv_x)
    def _():
        landed = prefix.at[pl.ds(0, (columns - 1) * part), :]
        remote(landed, landed, gather_send.at[0], gather_recv, layer=partner).wait_recv()
        swap.start()
        swap.wait_recv()

        @pl.when(send_e)
        def _():
            whole = prefix[...]
            jump[...] = (whole.astype(F32) + pair[...].astype(F32) + dot(whole, pair[...])).astype(BF16)

    def chunk(at):
        return pl.ds(pl.multiple_of(mine + at * step, step), step)

    shares = [
        remote(carried.at[chunk(at), :], carried.at[chunk(at), :], share_send.at[at], share_recv.at[at], layer=partner)
        for at in range(CHUNKS)
    ]

    @pl.when(first)
    def _():
        carried[...] = jnp.zeros_like(carried)

    @pl.when(both(neither(later), neither(first)))
    def _():
        for at, span in enumerate(spans):
            carried[chunk(at), :] = local_in[span, :]
            shares[at].start()

    def with_entering(at, span):
        here = e_in[span, :]

        @pl.when(opens)
        def _():
            carried[chunk(at), :] = here

        @pl.when(recv_local)
        def _():
            total = local_in[span, :].astype(F32) + here.astype(F32) + dot(here, prefix[...])
            carried[chunk(at), :] = total.astype(BF16)

        shares[at].start()

    @pl.when(both(later, send_e))
    def _():
        for at, span in enumerate(spans):
            e_hops[0][at].wait_recv()
            here = e_in[span, :]
            ahead = base[span, :] + here.astype(F32) + dot(here, jump[...])
            e_out[span, :] = ahead.astype(BF16)
            send_far(at)
        send_others()
        for at, span in enumerate(spans):
            with_entering(at, span)

    @pl.when(both(later, neither(send_e)))
    def _():
        for at, span in enumerate(spans):
            e_hops[0][at].wait_recv()
            with_entering(at, span)

    stores = []

    def finish(offset, slot):
        span = pl.ds(pl.multiple_of(offset, half), half)

        @pl.when(core == 0)
        def _():
            c_buf[span, :] = (state[span, :].astype(F32) + carried[span, :].astype(F32)).astype(BF16)

        @pl.when(both(core == 1, neither(first)))
        def _():
            here = carried[span, :]
            correction = here.astype(F32) + dot(here, maps[0]) + d_all[span, :]
            c_buf[span, :] = (state[span, :].astype(F32) + correction).astype(BF16)

        @pl.when(both(core == 1, first))
        def _():
            c_buf[span, :] = (state[span, :].astype(F32) + d_all[span, :]).astype(BF16)

        for buffer, out, at in ((c_buf, both_hbm.at[0], 0), (f_buf, both_hbm.at[1], 1)):
            stores.append(pltpu.make_async_copy(buffer.at[span, :], out.at[span, :], store_sem.at[2 * slot + at]))
        stores[-2].start()
        f_buf[span, :] = advance(c_buf[span, :], win[0], wout[0])
        stores[-1].start()

    finish(mine, 0)

    @pl.when(both(closes, neither(later)))
    def _():
        send_others()

    @pl.when(neither(first))
    def _():
        for share in shares:
            share.wait_recv()

    @pl.when(core == 1)
    def _():
        share_own.wait_recv()
        d_all[other_rows, :] = half_in[other_rows, :].astype(F32)

    finish(half - mine, 1)
    share_other.wait_send()

    @pl.when(core == 0)
    def _():
        share_own.wait_send()

    @pl.when(neither(first))
    def _():
        for share in shares:
            share.wait_send()

    @pl.when(send_map)
    def _():
        for hop in map_hops:
            hop.wait_send()
        for copy in to_before:
            copy.wait_send()

    @pl.when(send_x)
    def _():
        x_hop.wait_send()

    @pl.when(recv_x)
    def _():
        for gather in gathers:
            gather.wait_send()
        swap.wait_send()

    @pl.when(send_local)
    def _():
        for hop in local_hops:
            hop.wait_send()

    @pl.when(send_e)
    def _():
        for away in range(1, widest + 1):
            @pl.when(following_size >= away)
            def _(away=away):
                for hop in e_hops[away - 1]:
                    hop.wait_send()

    for store in stores:
        store.wait()


def shards(layers, columns, states, w_in, w_out):
    rows, width = states.shape[1:]
    hidden = w_in.shape[2]
    half = rows // 2
    part = width // (2 * columns)
    widest = max(groups_of(layers // 2)[1:])
    block = jax.ShapeDtypeStruct((rows, width), BF16)
    hbm = pl.BlockSpec(memory_space=pl.ANY)
    dma, vmem = pltpu.SemaphoreType.DMA, pltpu.VMEM
    result = pl.pallas_call(
        functools.partial(kernel, layers, columns),
        out_shape=jax.ShapeDtypeStruct((2, rows, width), BF16),
        in_specs=[hbm, hbm, hbm],
        out_specs=hbm,
        scratch_shapes=[
            vmem((rows, width), BF16),
            vmem((2, width, hidden), BF16),
            vmem((2, hidden, width), BF16),
            vmem((rows, width), BF16),
            vmem((2, width, width), BF16),
            vmem((width, width), BF16),
            vmem((rows, width), BF16),
            vmem((rows, width), F32),
            vmem((rows, width), BF16),
            vmem((rows, width), BF16),
            vmem((rows, width), F32),
            vmem((half, width), F32),
            vmem((rows, width), BF16),
            vmem((half, width), BF16),
            vmem((half, width), BF16),
            vmem((part, width), BF16),
            vmem((part, width), BF16),
            vmem((width, width), BF16),
            vmem((width, width), BF16),
            vmem((half, width), F32),
            vmem((half, width), BF16),
            vmem((half, width), BF16),
            vmem((rows, width), BF16),
            vmem((rows, width), BF16),
            dma((5,)),
            dma((2,)),
            dma((2,)),
            dma((2,)),
            dma((2,)),
            dma((2,)),
            dma((2,)),
            dma((2,)),
            dma((columns,)),
            dma,
            dma((2,)),
            dma((CHUNKS,)),
            dma((CHUNKS,)),
            dma((widest * CHUNKS,)),
            dma((CHUNKS,)),
            dma((CHUNKS,)),
            dma((CHUNKS,)),
            dma((4,)),
            pltpu.SemaphoreType.REGULAR,
            pltpu.SemaphoreType.REGULAR,
            pltpu.SemaphoreType.REGULAR,
        ],
        compiler_params=pltpu.CompilerParams(
            collective_id=0, has_side_effects=True, vmem_limit_bytes=67043328
        ),
    )(states[0], w_in, w_out)
    return (result[0:1], result[1:2])


def solution(mesh):
    return jax.shard_map(
        functools.partial(shards, mesh.shape["layer"], mesh.shape["dp"]),
        mesh=mesh,
        in_specs=(P("layer", "dp", None), P("layer", None, None), P("layer", None, None)),
        out_specs=(P("layer", "dp", None), P("layer", "dp", None)),
        check_vma=False,
    )
```

```python
import functools

import jax
import jax.numpy as jnp
from jax import lax
from jax.experimental import pallas as pl
from jax.experimental.pallas import tpu as pltpu
from jax.sharding import PartitionSpec as P

F32, BF16 = jnp.float32, jnp.bfloat16
ROOT_HALF = 0.7071067811865476
CHUNKS = 2


def groups_of(chips):
    if chips == 16:
        return (4, 4, 5, 3)
    return (chips // 3, chips // 3, chips - 2 * (chips // 3))


def dot(left, right):
    return jnp.dot(left, right, preferred_element_type=F32)


def gelu(x):
    return 0.5 * x * (1.0 + lax.erf(x * ROOT_HALF))


def advance(state, w_first, w_second):
    gated = gelu(dot(state, w_first)).astype(BF16)
    return (state.astype(F32) + 0.25 * dot(gated, w_second)).astype(BF16)


def kernel(
    layers, columns, states_hbm, win_hbm, wout_hbm, both_hbm,
    state, win, wout, follow, maps, pair, pushed, defect, half_out, half_in, d_all, b_half, carried,
    local_in, local_out, x_in, x_out, prefix, jump, base, e_in, e_out, c_buf, f_buf,
    load_sem, follow_send, follow_recv, map_send, map_recv, half_send, half_recv, x_sems, gather_send, gather_recv, swap_sems,
    local_send, local_recv, e_send, e_recv, share_send, share_recv, store_sem, hello, plane, in_plane,
):
    me, column = lax.axis_index("layer"), lax.axis_index("dp")
    core, chip = lax.rem(me, 2), me // 2
    partner = me + 1 - 2 * core
    rows, width = state.shape
    half, half_width = rows // 2, width // 2
    step = half // CHUNKS
    part = half_width // columns
    mine = core * half
    both, neither = jnp.logical_and, jnp.logical_not

    sizes = groups_of(layers // 2)
    widest = max(sizes[1:])
    start, size, following_size, at = 0, sizes[0], sizes[1], 0
    for k in range(1, len(sizes)):
        at += sizes[k - 1]
        reached = (chip >= at).astype(jnp.int32)
        ahead = sizes[k + 1] if k + 1 < len(sizes) else 0
        start = start + reached * sizes[k - 1]
        size = size + reached * (sizes[k] - sizes[k - 1])
        following_size = following_size + reached * (ahead - sizes[k])
    to_close = start + size - 1 - chip
    opens, closes = chip == start, to_close == 0
    later, first, last = chip >= sizes[0], chip == 0, chip == layers // 2 - 1
    recv_local, send_local = neither(opens), neither(closes)
    recv_x, send_x = both(recv_local, later), both(send_local, later)
    send_e = both(closes, following_size > 0)
    send_map, recv_map = me > 0, me != 1
    gate = both(closes, later)

    def number(flag):
        return flag.astype(jnp.int32)

    def remote(source, target, send, recv, **device):
        return pltpu.make_async_remote_copy(
            src_ref=source, dst_ref=target, send_sem=send, recv_sem=recv, device_id=device
        )

    loads = [
        pltpu.make_async_copy(source, target, load_sem.at[slot])
        for slot, (source, target) in enumerate((
            (states_hbm, state),
            (win_hbm.at[0], win.at[0]),
            (wout_hbm.at[0], wout.at[0]),
            (win_hbm.at[1], win.at[1]),
            (wout_hbm.at[1], wout.at[1]),
        ))
    ]
    for load in loads[:3]:
        load.start()

    barrier = pltpu.get_barrier_semaphore()
    send_back = both(core == 0, me > 0)
    recv_back = both(core == 1, me < layers - 1)

    def greet(**device):
        pl.semaphore_signal(barrier, inc=1, device_id=device)

    greet(layer=partner)

    @pl.when(recv_back)
    def _():
        greet(layer=me + 1)

    @pl.when(recv_local)
    def _():
        greet(layer=me - 2)

    @pl.when(both(later, neither(closes)))
    def _():
        greet(layer=me + 2 * to_close)

    @pl.when(send_e)
    def _():
        greet(layer=me + 2 * following_size)

    side = 4 if columns % 4 == 0 else 1
    depth = columns // side
    line, place = column // depth, lax.rem(column, depth)
    in_line = [line * depth + lax.rem(place + turn, depth) for turn in range(1, depth)]
    across = [lax.rem(line + turn, side) * depth + place for turn in range(1, side)]

    @pl.when(gate)
    def _():
        for peer in in_line + across:
            greet(dp=peer)

    loads[0].wait()
    for load in loads[3:]:
        load.start()
    low, high = pl.ds(0, half_width), pl.ds(half_width, half_width)

    def make_map(span):
        maps[core, span, :] = (0.25 * dot(win[0, span, :], wout[0])).astype(BF16)

    @pl.when(gate)
    def _():
        loads[1].wait()
        loads[2].wait()
        make_map(low)
        make_map(high)

    pl.semaphore_wait(
        barrier,
        1 + number(send_back) + number(send_local) + number(gate) * (size + len(in_line) + len(across)),
    )

    def half_at(offset):
        return pl.ds(pl.multiple_of(offset, half), half)

    own_rows, other_rows = half_at(mine), half_at(half - mine)
    to_before = [
        remote(state.at[span, :], follow.at[span, :], follow_send.at[at], follow_recv.at[at], layer=me - 1)
        for at, span in enumerate((own_rows, other_rows))
    ]

    map_hops = [
        remote(maps.at[core, span, :], maps.at[core, span, :], map_send.at[at], map_recv.at[at], layer=partner)
        for at, span in enumerate((low, high))
    ]

    @pl.when(gate)
    def _():
        for hop in map_hops:
            hop.start()

    @pl.when(me > 0)
    def _():
        for copy in to_before:
            copy.start()

    @pl.when(neither(gate))
    def _():
        loads[1].wait()
        loads[2].wait()

        @pl.when(send_map)
        def _():
            for span, hop in zip((low, high), map_hops):
                make_map(span)
                hop.start()

    @pl.when(gate)
    def _():
        pl.semaphore_signal(hello, inc=1, device_id={"layer": 2 * (start - 1) + core})
        for peer in in_line:
            pl.semaphore_signal(in_plane, inc=1, device_id={"dp": peer})

    relaxed = advance(state[...], win[0], wout[0])

    loads[3].wait()
    loads[4].wait()
    pushed[...] = advance(relaxed, win[1], wout[1])
    share_other, share_own = [
        remote(half_out.at[span, :], half_in.at[span, :], half_send.at[at], half_recv.at[at], layer=partner)
        for at, span in enumerate((other_rows, own_rows))
    ]

    @pl.when(me == layers - 1)
    def _():
        follow[...] = jnp.zeros_like(follow)

    def take_defect(at, span):
        @pl.when(me < layers - 1)
        def _():
            to_before[at].wait_recv()

        defect[span, :] = pushed[span, :].astype(F32) - follow[span, :].astype(F32)
        half_out[span, :] = defect[span, :].astype(BF16)

    take_defect(0, other_rows)
    share_other.start()
    take_defect(1, own_rows)

    @pl.when(core == 0)
    def _():
        share_own.start()

    @pl.when(gate)
    def _():
        if in_line:
            pl.semaphore_wait(in_plane, len(in_line))
        for peer in across:
            pl.semaphore_signal(plane, inc=1, device_id={"dp": peer})

    @pl.when(recv_map)
    def _():
        for hop in map_hops:
            hop.wait_recv()

    def pair_rows(span):
        ahead = maps[0, span, :].astype(F32) + maps[1, span, :].astype(F32)
        return (ahead + dot(maps[0, span, :], maps[1])).astype(BF16)

    own_part = pl.ds(pl.multiple_of(core * half_width + column * part, part), part)
    x_hop = remote(x_out, x_in, x_sems.at[0], x_sems.at[1], layer=me + 2)
    peers = [lax.rem(column + turn, columns) for turn in range(1, columns)]
    gathers = [
        remote(x_in, prefix.at[own_part, :], gather_send.at[turn], gather_recv, dp=peer)
        for turn, peer in enumerate(peers)
    ]
    half_prefix = prefix.at[pl.ds(pl.multiple_of(core * half_width, half_width), half_width), :]
    swap = remote(half_prefix, half_prefix, swap_sems.at[0], swap_sems.at[1], layer=partner)

    @pl.when(both(send_x, opens))
    def _():
        x_out[...] = pair_rows(own_part)
        x_hop.start()

    @pl.when(neither(first))
    def _():
        pair[...] = pair_rows(pl.ds(0, width))

    @pl.when(gate)
    def _():
        if across:
            pl.semaphore_wait(plane, len(across))
        for turn in range(1, widest - 1):
            @pl.when(turn < size - 1)
            def _(turn=turn):
                pl.semaphore_signal(plane, inc=1, device_id={"layer": me - 2 * turn})

    @pl.when(recv_x)
    def _():
        x_hop.wait_recv()

        @pl.when(send_x)
        def _():
            x = x_in[...]
            x_out[...] = (pair[own_part, :].astype(F32) + x.astype(F32) + dot(x, pair[...])).astype(BF16)
            x_hop.start()

        @pl.when(send_x)
        def _():
            pl.semaphore_wait(plane, 1)

        for gather in gathers:
            gather.start()
        prefix[own_part, :] = x_in[...]

    share_other.wait_recv()

    @pl.when(core == 0)
    def _():
        d_all[own_rows, :] = defect[own_rows, :]
        b_half[...] = half_in[own_rows, :].astype(F32)

    @pl.when(core == 1)
    def _():
        d_all[own_rows, :] = half_in[own_rows, :].astype(F32)
        b_half[...] = defect[own_rows, :]

    even_half = d_all[own_rows, :]
    b_half[...] += even_half + dot(even_half.astype(BF16), maps[1])

    spans = [pl.ds(at * step, step) for at in range(CHUNKS)]
    local_hops = [
        remote(local_out.at[span, :], local_in.at[span, :], local_send.at[at], local_recv.at[at], layer=me + 2)
        for at, span in enumerate(spans)
    ]
    e_hops = [
        [
            remote(
                e_out.at[span, :], e_in.at[span, :], e_send.at[(away - 1) * CHUNKS + at], e_recv.at[at],
                layer=me + 2 * away,
            )
            for at, span in enumerate(spans)
        ]
        for away in range(1, widest + 1)
    ]

    def send_far(at):
        if at == 0:
            pl.semaphore_wait(hello, 1)
        for away in range(1, widest + 1):
            @pl.when(following_size == away)
            def _(away=away):
                e_hops[away - 1][at].start()

    def send_others():
        for away in range(widest - 1, 0, -1):
            @pl.when(following_size > away)
            def _(away=away):
                for hop in e_hops[away - 1]:
                    hop.start()

    @pl.when(both(opens, send_local))
    def _():
        local_out[...] = b_half[...].astype(BF16)
        for hop in local_hops:
            hop.start()

    @pl.when(recv_local)
    def _():
        for at, span in enumerate(spans):
            local_hops[at].wait_recv()

            @pl.when(neither(last))
            def _(at=at, span=span):
                here = local_in[span, :]
                ahead = here.astype(F32) + dot(here, pair[...]) + b_half[span, :]

                @pl.when(send_local)
                def _():
                    local_out[span, :] = ahead.astype(BF16)
                    local_hops[at].start()

                @pl.when(both(closes, later))
                def _():
                    base[span, :] = ahead

                @pl.when(both(closes, neither(later)))
                def _():
                    e_out[span, :] = ahead.astype(BF16)
                    send_far(at)

    @pl.when(recv_x)
    def _():
        landed = prefix.at[pl.ds(0, (columns - 1) * part), :]
        remote(landed, landed, gather_send.at[0], gather_recv, layer=partner).wait_recv()
        swap.start()
        swap.wait_recv()

        @pl.when(send_e)
        def _():
            whole = prefix[...]
            jump[...] = (whole.astype(F32) + pair[...].astype(F32) + dot(whole, pair[...])).astype(BF16)

    def chunk(at):
        return pl.ds(pl.multiple_of(mine + at * step, step), step)

    shares = [
        remote(carried.at[chunk(at), :], carried.at[chunk(at), :], share_send.at[at], share_recv.at[at], layer=partner)
        for at in range(CHUNKS)
    ]

    @pl.when(first)
    def _():
        carried[...] = jnp.zeros_like(carried)

    @pl.when(both(neither(later), neither(first)))
    def _():
        for at, span in enumerate(spans):
            carried[chunk(at), :] = local_in[span, :]
            shares[at].start()

    def with_entering(at, span):
        here = e_in[span, :]

        @pl.when(opens)
        def _():
            carried[chunk(at), :] = here

        @pl.when(recv_local)
        def _():
            total = local_in[span, :].astype(F32) + here.astype(F32) + dot(here, prefix[...])
            carried[chunk(at), :] = total.astype(BF16)

        shares[at].start()

    @pl.when(both(later, send_e))
    def _():
        for at, span in enumerate(spans):
            e_hops[0][at].wait_recv()
            here = e_in[span, :]
            ahead = base[span, :] + here.astype(F32) + dot(here, jump[...])
            e_out[span, :] = ahead.astype(BF16)
            send_far(at)
        send_others()
        for at, span in enumerate(spans):
            with_entering(at, span)

    @pl.when(both(later, neither(send_e)))
    def _():
        for at, span in enumerate(spans):
            e_hops[0][at].wait_recv()
            with_entering(at, span)

    stores = []

    def finish(offset, slot):
        span = pl.ds(pl.multiple_of(offset, half), half)

        @pl.when(core == 0)
        def _():
            c_buf[span, :] = (state[span, :].astype(F32) + carried[span, :].astype(F32)).astype(BF16)

        @pl.when(both(core == 1, neither(first)))
        def _():
            here = carried[span, :]
            correction = here.astype(F32) + dot(here, maps[0]) + d_all[span, :]
            c_buf[span, :] = (state[span, :].astype(F32) + correction).astype(BF16)

        @pl.when(both(core == 1, first))
        def _():
            c_buf[span, :] = (state[span, :].astype(F32) + d_all[span, :]).astype(BF16)

        for buffer, out, at in ((c_buf, both_hbm.at[0], 0), (f_buf, both_hbm.at[1], 1)):
            stores.append(pltpu.make_async_copy(buffer.at[span, :], out.at[span, :], store_sem.at[2 * slot + at]))
        stores[-2].start()
        f_buf[span, :] = advance(c_buf[span, :], win[0], wout[0])
        stores[-1].start()

    finish(mine, 0)

    @pl.when(both(closes, neither(later)))
    def _():
        send_others()

    @pl.when(neither(first))
    def _():
        for share in shares:
            share.wait_recv()

    @pl.when(core == 1)
    def _():
        share_own.wait_recv()
        d_all[other_rows, :] = half_in[other_rows, :].astype(F32)

    finish(half - mine, 1)
    share_other.wait_send()

    @pl.when(core == 0)
    def _():
        share_own.wait_send()

    @pl.when(neither(first))
    def _():
        for share in shares:
            share.wait_send()

    @pl.when(send_map)
    def _():
        for hop in map_hops:
            hop.wait_send()
        for copy in to_before:
            copy.wait_send()

    @pl.when(send_x)
    def _():
        x_hop.wait_send()

    @pl.when(recv_x)
    def _():
        for gather in gathers:
            gather.wait_send()
        swap.wait_send()

    @pl.when(send_local)
    def _():
        for hop in local_hops:
            hop.wait_send()

    @pl.when(send_e)
    def _():
        for away in range(1, widest + 1):
            @pl.when(following_size >= away)
            def _(away=away):
                for hop in e_hops[away - 1]:
                    hop.wait_send()

    for store in stores:
        store.wait()


def shards(layers, columns, states, w_in, w_out):
    rows, width = states.shape[1:]
    hidden = w_in.shape[2]
    half = rows // 2
    part = width // (2 * columns)
    widest = max(groups_of(layers // 2)[1:])
    block = jax.ShapeDtypeStruct((rows, width), BF16)
    hbm = pl.BlockSpec(memory_space=pl.ANY)
    dma, vmem = pltpu.SemaphoreType.DMA, pltpu.VMEM
    result = pl.pallas_call(
        functools.partial(kernel, layers, columns),
        out_shape=jax.ShapeDtypeStruct((2, rows, width), BF16),
        in_specs=[hbm, hbm, hbm],
        out_specs=hbm,
        scratch_shapes=[
            vmem((rows, width), BF16),
            vmem((2, width, hidden), BF16),
            vmem((2, hidden, width), BF16),
            vmem((rows, width), BF16),
            vmem((2, width, width), BF16),
            vmem((width, width), BF16),
            vmem((rows, width), BF16),
            vmem((rows, width), F32),
            vmem((rows, width), BF16),
            vmem((rows, width), BF16),
            vmem((rows, width), F32),
            vmem((half, width), F32),
            vmem((rows, width), BF16),
            vmem((half, width), BF16),
            vmem((half, width), BF16),
            vmem((part, width), BF16),
            vmem((part, width), BF16),
            vmem((width, width), BF16),
            vmem((width, width), BF16),
            vmem((half, width), F32),
            vmem((half, width), BF16),
            vmem((half, width), BF16),
            vmem((rows, width), BF16),
            vmem((rows, width), BF16),
            dma((5,)),
            dma((2,)),
            dma((2,)),
            dma((2,)),
            dma((2,)),
            dma((2,)),
            dma((2,)),
            dma((2,)),
            dma((columns,)),
            dma,
            dma((2,)),
            dma((CHUNKS,)),
            dma((CHUNKS,)),
            dma((widest * CHUNKS,)),
            dma((CHUNKS,)),
            dma((CHUNKS,)),
            dma((CHUNKS,)),
            dma((4,)),
            pltpu.SemaphoreType.REGULAR,
            pltpu.SemaphoreType.REGULAR,
            pltpu.SemaphoreType.REGULAR,
        ],
        compiler_params=pltpu.CompilerParams(
            collective_id=0, has_side_effects=True, vmem_limit_bytes=67043328
        ),
    )(states[0], w_in, w_out)
    return (result[0:1], result[1:2])


def solution(mesh):
    return jax.shard_map(
        functools.partial(shards, mesh.shape["layer"], mesh.shape["dp"]),
        mesh=mesh,
        in_specs=(P("layer", "dp", None), P("layer", None, None), P("layer", None, None)),
        out_specs=(P("layer", "dp", None), P("layer", "dp", None)),
        check_vma=False,
    )
```
